256 devices in a mesh: leaf: 16 (over z, core), prow: 4 (over x), pcol: 4 (over y).
Axes of the slice: x: 4, y: 4, z: 8, core: 2. Of those that a mesh axis runs over, the one named last changes fastest.
Arguments:
- child_inverse: float32 [256, 512, 512], P(('leaf', 'prow', 'pcol')), parts along dimension 0, as said below
- child_coupling: float32 [256, 1024, 512], P(('leaf', 'prow', 'pcol')), parts along dimension 0, may hold values from -0.25 to 0.25
- child_blocks: int32 [256], P(('leaf', 'prow', 'pcol')), parts along dimension 0, may hold values from 2 to 8, as said below
- child_map: int32 [256, 8], P(('leaf', 'prow', 'pcol')), parts along dimension 0, may hold values from -1 to 15, as said below
- parent_front: float32 [32768, 2048], P(('leaf', 'prow'), 'pcol'), parts along dimension 0, as said below
Outputs:
- parent_factored: float32 [32768, 2048], P(('leaf', 'prow'), 'pcol'), parts along dimension 0
The draws below stay inside these ranges and needn't reach their ends.
There are 16 independent parts, one for each index of `leaf`. The reference program is written for one: setup_inputs(seed, part) draws one part's arguments, and reference() takes and returns one part's arrays. A program takes and returns all parts, laid end to end along the dimension named above; each array names one. Nothing has to cross between parts.
Inputs may be any that keep to these rules, and one draw needn't show every extreme that they name: `child_inverse`: each matrix is lower triangular with a positive diagonal. `child_blocks`: the largest value 8 is taken by some child in every draw. `child_map`: in row c the first child_blocks[c] entries are distinct parent block ids in increasing order and the others are -1. `parent_front`: symmetric; the assembled front is positive definite.
All inputs are finite; a program needn't handle non-finite values.
Results may differ from the reference program's by a relative error of at most 0.0003.
Values sent between devices are 32-bit elements; how exact they have to be, the bound alone decides.
A program may use at most 128 MiB of HBM per device.

```python
import math
import jax
import jax.numpy as jnp
from jax import lax

P_SIZE = 512
SMAX = 1024
BLK = 128
PORD = 2048
NCHILD = 16
PANEL = 512


def child_layout(key):
    folded = jax.random.fold_in(key, 7)
    slot_count = SMAX // BLK
    block_total = PORD // BLK
    blocks = jax.random.randint(jax.random.fold_in(folded, 1), (NCHILD,), 2, slot_count + 1)
    chosen = jax.random.randint(jax.random.fold_in(folded, 2), (), 0, NCHILD)
    blocks = jnp.where(jnp.arange(NCHILD) == chosen, slot_count, blocks)
    child_keys = jax.random.split(jax.random.fold_in(folded, 3), NCHILD)
    shuffled = jax.vmap(lambda one_key: jax.random.permutation(one_key, block_total))(child_keys)[:, :slot_count]
    in_use = jnp.arange(slot_count)[None, :] < blocks[:, None]
    sorted_ids = jnp.sort(jnp.where(in_use, shuffled, block_total), axis=1)
    mapping = jnp.where(sorted_ids < block_total, sorted_ids, -1)
    return (blocks.astype(jnp.int32), mapping.astype(jnp.int32))


def draw_child_blocks(key, part):
    return child_layout(key)[0]


def draw_child_map(key, part):
    return child_layout(key)[1]


def draw_child_inverse(key, part):
    first_key, second_key = jax.random.split(jax.random.fold_in(key, 11))
    raw_noise = jax.random.truncated_normal(first_key, -4.0, 4.0, (NCHILD, P_SIZE, P_SIZE), jnp.float32)
    diagonal = jnp.exp(jax.random.uniform(second_key, (NCHILD, P_SIZE), jnp.float32, math.log(0.35), math.log(0.65)))
    row_ids = jnp.arange(P_SIZE)[:, None]
    col_ids = jnp.arange(P_SIZE)[None, :]
    below = (row_ids > col_ids).astype(jnp.float32)
    identity = (row_ids == col_ids).astype(jnp.float32)
    return raw_noise * below[None, :, :] * (0.2 / math.sqrt(P_SIZE)) + identity[None, :, :] * diagonal[:, None, :]


def gram_front(key, order, gram_scale, low_ridge, high_ridge):
    first_key, second_key = jax.random.split(key)
    factor_noise = jax.random.truncated_normal(first_key, -4.0, 4.0, (order, order), jnp.float32)
    ridge = jnp.exp(jax.random.uniform(second_key, (order,), jnp.float32, math.log(low_ridge), math.log(high_ridge)))
    gram = jnp.dot(factor_noise, factor_noise.T, precision=lax.Precision.HIGHEST, preferred_element_type=jnp.float32) * (gram_scale / order)
    gram = 0.5 * (gram + gram.T)
    identity = jnp.eye(order, dtype=jnp.float32)
    return gram + identity * ridge[None, :]


def draw_parent_front(key, part):
    return gram_front(jax.random.fold_in(key, 13), PORD, 16.0, 4.0, 10.0)


def shard_levels(own_key, extent, cuts, least, top_value):
    loudness = 1.0
    for axis_at, parts in cuts:
        draws = jax.random.uniform(jax.random.fold_in(jax.random.fold_in(own_key, 6), axis_at), (parts,), jnp.float32, least / len(cuts), top_value / len(cuts))
        loudness = loudness * jnp.repeat(jnp.exp(draws), extent[axis_at] // parts).reshape((-1,) + (1,) * (len(extent) - 1 - axis_at))
    return loudness


def scatter_about(rng, extent, scale, bound, shards=(), kind=jnp.bfloat16):
    level = shard_levels(rng, extent, shards, -0.22, 0.18) if shards else 1.0
    entries = jax.random.normal(rng, extent, jnp.float32) * scale * level
    return jnp.minimum(jnp.maximum(entries, -bound), bound).astype(kind)


def setup_inputs(seed: int = 0, part: int = 0) -> dict:
    splits = jax.random.split(jax.random.key(seed), 6)
    part_splits = jax.random.split(jax.random.fold_in(splits[5], part), 6)
    return {
        "child_inverse": draw_child_inverse(jax.random.fold_in(jax.random.fold_in(splits[5], part), 71), part),
        "child_coupling": scatter_about(part_splits[1], (NCHILD, SMAX, P_SIZE), P_SIZE ** -0.5, 0.25, ((0, 16),), jnp.float32),
        "child_blocks": draw_child_blocks(jax.random.fold_in(jax.random.fold_in(splits[5], part), 71), part),
        "child_map": draw_child_map(jax.random.fold_in(jax.random.fold_in(splits[5], part), 71), part),
        "parent_front": draw_parent_front(jax.random.fold_in(jax.random.fold_in(splits[5], part), 71), part),
    }


def child_update(inverse_block, coupling, blocks, mapping):
    row_ids = jnp.arange(SMAX)
    masked = jnp.where((row_ids < blocks * BLK)[:, None], coupling, jnp.zeros_like(coupling))
    factor = jnp.dot(masked.astype(jnp.float32), inverse_block.T.astype(jnp.float32), precision=lax.Precision.HIGHEST, preferred_element_type=jnp.float32)
    update = jnp.dot(factor.astype(jnp.float32), factor.T.astype(jnp.float32), precision=lax.Precision.HIGHEST, preferred_element_type=jnp.float32)
    select = (mapping[None, :] == jnp.arange(PORD // BLK)[:, None]).astype(jnp.float32)
    blocked = update.reshape(SMAX // BLK, BLK, SMAX // BLK, BLK)
    spread = jnp.einsum('bk,kiln,dl->bidn', select, blocked, select, precision=lax.Precision.HIGHEST)
    return spread.reshape(PORD, PORD)

def reference(child_inverse, child_coupling, child_blocks, child_map, parent_front):

    def accumulate(summed, child_items):
        return (summed + child_update(*child_items), None)
    summed, unused = lax.scan(accumulate, jnp.zeros((PORD, PORD), jnp.float32), (child_inverse, child_coupling, child_blocks, child_map))
    assembled = parent_front - summed
    diag_factor = jnp.linalg.cholesky(assembled[:PANEL, :PANEL])
    solved = lax.linalg.triangular_solve(diag_factor, assembled[:, :PANEL], left_side=False, lower=True, transpose_a=True)
    panel_rows = jnp.concatenate([diag_factor, solved[PANEL:]], 0)
    below = panel_rows[PANEL:]
    trailing = assembled[PANEL:, PANEL:] - jnp.dot(below.astype(jnp.float32), below.T.astype(jnp.float32), precision=lax.Precision.HIGHEST, preferred_element_type=jnp.float32)
    upper_right = assembled[:PANEL, PANEL:]
    right_side = jnp.concatenate([upper_right, trailing], 0)
    return jnp.concatenate([panel_rows, right_side], 1)
```

```python
import functools

import jax
import jax.numpy as jnp
from jax import lax
from jax.experimental import pallas as pl
from jax.experimental.pallas import tpu as pltpu
from jax.sharding import PartitionSpec as P

BLK = 128
TILE = 512
NT = 10
GROUPS = ((0, 1), (1, 3), (4, 3), (7, 3))
OWNERS = ((1, 1), (2, 1), (3, 1), (2, 2), (3, 2), (3, 3))
AXES = ("prow", "pcol")
F32 = jnp.float32
BF16 = jnp.bfloat16
DN_NT = (((1,), (1,)), ((), ()))


def split(x):
    hi = x.astype(BF16)
    return hi, (x - hi.astype(F32)).astype(BF16)


def dot_nt(a, b):
    return lax.dot_general(a, b, DN_NT, preferred_element_type=F32)


def dot3(a, b):
    return dot_nt(a[0], b[0]) + dot_nt(a[0], b[1]) + dot_nt(a[1], b[0])


def mm_nt(a, b):
    return dot3(split(a), split(b))


def kernel(slot_ref, inv_ref, coup_ref, parent_ref, out_ref,
           fac_h, fac_l, fh, fl, s_buf, rl1, rf1, rl2, rf2, w_buf, z_buf, t_buf,
           ch, md, linv, p_buf,
           send_sem, recv_sem, dist_send, dist_recv):
    ci = lax.axis_index("prow")
    cj = lax.axis_index("pcol")
    coord = {"prow": ci, "pcol": cj}

    def nxt(v, k):
        return lax.rem(v + k, 4)

    barrier = pltpu.get_barrier_semaphore()
    for dx in range(4):
        for dy in range(4):
            if dx or dy:
                pl.semaphore_signal(
                    barrier, inc=1,
                    device_id={"prow": nxt(ci, dx), "pcol": nxt(cj, dy)},
                    device_id_type=pl.DeviceIdType.MESH)

    ih, il = split(inv_ref[...])

    @pl.loop(0, 8)
    def _(s):
        c = split(coup_ref[pl.ds(pl.multiple_of(s * BLK, BLK), BLK), :])
        f = dot3(c, (ih, il))
        h, l = split(f)
        fac_h[s] = h
        fac_l[s] = l

    @pl.loop(0, 16)
    def _(b):
        s = slot_ref[b]
        ok = slot_ref[16 + b] > 0
        h = fac_h[s]
        l = fac_l[s]
        rows = pl.ds(pl.multiple_of(b * BLK, BLK), BLK)
        fh[rows, :] = jnp.where(ok, h, jnp.zeros_like(h))
        fl[rows, :] = jnp.where(ok, l, jnp.zeros_like(l))

    def tile(r, col, t):
        rows = pl.ds(pl.multiple_of(r * TILE, TILE), TILE)
        cols = pl.ds(col * TILE, TILE)
        d = dot3((fh[rows, :], fl[rows, :]), (fh[cols, :], fl[cols, :]))
        if col == 0:
            mine = jnp.logical_and(ci == r, cj == 0)
            d = d - jnp.where(mine, parent_ref[...], jnp.zeros((TILE, TILE), F32))
        for c in range(2):
            for a in range(4):
                o = c * 256 + a * 64
                s_buf[c, a, t] = d[o:o + 64]

    def tiles(col, lo, hi, base):
        @pl.loop(lo, hi)
        def _(r):
            tile(r, col, base + r)

    def copy(src, dst, g, c, d, kind, axis, k):
        return pltpu.make_async_remote_copy(
            src_ref=src, dst_ref=dst,
            send_sem=send_sem.at[g, c, d, kind], recv_sem=recv_sem.at[g, c, d, kind],
            device_id={axis: nxt(coord[axis], k)}, device_id_type=pl.DeviceIdType.MESH)

    started = []

    def go(cp):
        cp.start()
        started.append(cp)

    STEP = (1, 3)

    def rs(g, c, phase):
        t0, n = GROUPS[g]
        ts = pl.ds(t0, n)
        first, second = AXES[c], AXES[1 - c]
        m = coord[first]
        if phase == 1:
            axis, me, half = first, m, 32
            rl, rf, kb = rl1, rf1, 0

            def chunk(d, h):
                return s_buf.at[c, d, ts, pl.ds(h * 32, 32)]
        else:
            axis, me, half = second, coord[second], 8
            rl, rf, kb = rl2, rf2, 3

            def chunk(d, h):
                return s_buf.at[c, m, ts, pl.ds(pl.multiple_of(d * 16 + h * 8, 8), 8)]
        relay = [copy(chunk(nxt(me, 2), 1 - d), rl.at[c, d, ts], g, c, d, kb, axis, STEP[d])
                 for d in range(2)]
        raw = [copy(chunk(nxt(me, STEP[d]), d), rf.at[c, d, ts, pl.ds(d * half, half)], g, c, d, kb + 1, axis, STEP[d])
               for d in range(2)]
        fin = [copy(chunk(nxt(me, STEP[d]), 1 - d), rf.at[c, d, ts, pl.ds((1 - d) * half, half)], g, c, d, kb + 2, axis, STEP[d])
               for d in range(2)]
        return relay, raw, fin, chunk, me, rl, rf

    def rs_start(g, phase):
        for c in range(2):
            relay, raw, *_ = rs(g, c, phase)
            for d in range(2):
                go(relay[d])
            for d in range(2):
                go(raw[d])

    def rs_relay(g, phase):
        t0, n = GROUPS[g]
        for c in range(2):
            relay, raw, fin, chunk, me, rl, rf = rs(g, c, phase)
            for d in range(2):
                relay[d].wait_recv()
                ref = chunk(nxt(me, STEP[d]), 1 - d)
                ref[...] = ref[...] + rl[c, d, t0:t0 + n]
                go(fin[d])

    def rs_final(g, phase):
        t0, n = GROUPS[g]
        for c in range(2):
            relay, raw, fin, chunk, me, rl, rf = rs(g, c, phase)
            for d in range(2):
                raw[d].wait_recv()
                fin[d].wait_recv()
            m = coord[AXES[c]]
            if phase == 1:
                for t in range(t0, t0 + n):
                    s_buf[c, m, t] = s_buf[c, m, t] + rf[c, 0, t] + rf[c, 1, t]
            else:
                rows = pl.ds(pl.multiple_of(me * 16, 16), 16)
                for t in range(t0, t0 + n):
                    z = s_buf[c, m, t, rows, :] + rf[c, 0, t] + rf[c, 1, t]
                    if g < 2:
                        w_buf[c, m, t, rows, :] = z
                    else:
                        z_buf[c, t - 4] = z

    def ag(g, c, phase):
        t0, n = GROUPS[g]
        ts = pl.ds(t0, n)
        first, second = AXES[c], AXES[1 - c]
        m = coord[first]
        if phase == 3:
            axis, me, kb = second, coord[second], 6

            def part(v, h, k):
                return w_buf.at[c, m, ts, pl.ds(pl.multiple_of(v * 16 + h * 8, 8), k * 8)]
        else:
            axis, me, kb = first, m, 8

            def part(v, h, k):
                return w_buf.at[c, v, ts, pl.ds(h * 32, k * 32)]
        own = []
        own_in = []
        fwd = []
        fwd_in = []
        for d in range(2):
            src = part(me, 0, 2)
            own.append(copy(src, src, g, c, d, kb, axis, STEP[d]))
            inc = part(nxt(me, STEP[1 - d]), 0, 2)
            own_in.append(copy(inc, inc, g, c, d, kb, axis, STEP[d]))
            f = part(nxt(me, STEP[1 - d]), d, 1)
            fwd.append(copy(f, f, g, c, d, kb + 1, axis, STEP[d]))
            fi = part(nxt(me, 2), d, 1)
            fwd_in.append(copy(fi, fi, g, c, d, kb + 1, axis, STEP[d]))
        return own, own_in, fwd, fwd_in

    def ag_start(g, phase):
        for c in range(2):
            for cp in ag(g, c, phase)[0]:
                go(cp)

    def ag_forward(g, phase):
        for c in range(2):
            own, own_in, fwd, fwd_in = ag(g, c, phase)
            for d in range(2):
                own_in[d].wait_recv()
                go(fwd[d])

    def ag_final(g, phase):
        for c in range(2):
            own, own_in, fwd, fwd_in = ag(g, c, phase)
            for d in range(2):
                fwd_in[d].wait_recv()

    deliveries = []

    def deliver(g):
        t0, n = GROUPS[g]
        for t in range(t0 - 4, t0 - 4 + n):
            r, q = OWNERS[t]
            for k, (x, y) in enumerate(((r, q), (q, r))[: 1 if r == q else 2]):
                mine = jnp.logical_and(ci == x, cj == y)
                for c in range(2):
                    m = coord[AXES[c]]
                    v = coord[AXES[1 - c]]
                    rows = pl.ds(pl.multiple_of(c * 256 + m * 64 + v * 16, 16), 16)
                    cp = pltpu.make_async_remote_copy(
                        src_ref=z_buf.at[c, t], dst_ref=t_buf.at[rows],
                        send_sem=dist_send.at[t, k, c], recv_sem=dist_recv.at[0],
                        device_id={"prow": x, "pcol": y}, device_id_type=pl.DeviceIdType.MESH)

                    @pl.when(mine)
                    def _():
                        t_buf[rows, :] = z_buf[c, t]

                    @pl.when(jnp.logical_not(mine))
                    def _():
                        cp.start()
                    deliveries.append((mine, cp))

    def chol_begin(kb):
        o = kb * BLK
        eye = lax.broadcasted_iota(jnp.int32, (BLK, BLK), 0) == lax.broadcasted_iota(jnp.int32, (BLK, BLK), 1)
        md[:, 0:BLK] = ch[o:o + BLK, o:o + BLK]
        md[:, BLK:2 * BLK] = eye.astype(F32)

    def chol_chunk(q):
        lo = q * 32
        x = md[lo:BLK, 0:BLK]
        y = md[lo:BLK, BLK:2 * BLK]
        rid = lax.broadcasted_iota(jnp.int32, (BLK - lo, BLK), 0)
        for k in range(32):
            row = x[k:k + 1, :]
            col = jnp.broadcast_to(x[:, lo + k:lo + k + 1], x.shape)
            piv = col[k:k + 1, :]
            inv = 1.0 / piv
            mul = jnp.where(rid > k, col, 0.0)
            x = x - mul * (row * inv)
            y = y - mul * (y[k:k + 1, :] * inv)
        md[lo:BLK, 0:BLK] = x
        md[lo:BLK, BLK:2 * BLK] = y

    def chol_end(kb):
        o = kb * BLK
        ri = lax.broadcasted_iota(jnp.int32, (BLK, BLK), 0)
        cj_ = lax.broadcasted_iota(jnp.int32, (BLK, BLK), 1)
        u = md[:, 0:BLK]
        piv = jnp.sum(jnp.where(ri == cj_, u, 0.0), axis=1, keepdims=True)
        sc = lax.rsqrt(piv)
        li = md[:, BLK:2 * BLK] * sc
        linv[kb] = li
        low = jnp.where(cj_ >= ri, u * sc, 0.0).T
        ch[o:o + BLK, o:o + BLK] = low
        if kb < 3:
            lp = lax.dot_general(ch[o + BLK:, o:o + BLK], li, DN_NT, precision=lax.Precision.HIGHEST,
                                 preferred_element_type=F32)
            ch[o + BLK:, o:o + BLK] = lp
            ch[o + BLK:, o + BLK:] = ch[o + BLK:, o + BLK:] - lax.dot_general(
                lp, lp, DN_NT, precision=lax.Precision.HIGHEST, preferred_element_type=F32)
            ch[o:o + BLK, o + BLK:] = jnp.zeros((BLK, TILE - o - BLK), F32)

    def solve(x, idx):
        @pl.loop(0, 2)
        def _(c):
            a = -jnp.reshape(w_buf[c, :, pl.ds(idx, 1)], (256, TILE))
            rows = pl.ds(pl.multiple_of(c * 256, 256), 256)
            for b in range(4):
                o = b * BLK
                v = a[:, o:o + BLK]
                if b:
                    v = v - mm_nt(p_buf[x, rows, 0:o], ch[o:o + BLK, 0:o])
                p_buf[x, rows, o:o + BLK] = mm_nt(v, linv[b])

    tiles(0, 0, 1, 0)
    pl.semaphore_wait(barrier, 15)
    rs_start(0, 1)
    tiles(0, 1, 4, 0)
    rs_start(1, 1)
    rs_relay(0, 1)
    rs_final(0, 1)
    rs_start(0, 2)
    tiles(1, 1, 4, 3)
    rs_relay(0, 2)
    rs_relay(1, 1)
    rs_final(0, 2)
    ag_start(0, 3)
    rs_start(2, 1)
    ag_forward(0, 3)
    ag_final(0, 3)
    ag_start(0, 4)
    rs_final(1, 1)
    rs_start(1, 2)
    ag_forward(0, 4)
    tiles(2, 2, 4, 5)
    tiles(3, 3, 4, 6)
    rs_relay(1, 2)
    rs_relay(2, 1)
    ag_final(0, 4)
    for c in range(2):
        for a in range(4):
            o = c * 256 + a * 64
            ch[o:o + 64, :] = -w_buf[c, a, 0]

    def chol(kb, events):
        chol_begin(kb)
        for q in range(4):
            chol_chunk(q)
            for e in events[q]:
                e()
        chol_end(kb)

    P_ = functools.partial
    rs_final(1, 2)
    ag_start(1, 3)
    rs_start(3, 1)
    chol(0, ((P_(ag_forward, 1, 3), P_(ag_final, 1, 3), P_(ag_start, 1, 4)),
             (P_(rs_final, 2, 1), P_(rs_start, 2, 2)),
             (P_(rs_relay, 2, 2), P_(rs_relay, 3, 1)),
             (P_(ag_forward, 1, 4),)))
    chol(1, ((P_(rs_final, 2, 2), P_(deliver, 2)),
             (P_(rs_final, 3, 1), P_(rs_start, 3, 2)),
             (P_(rs_relay, 3, 2),),
             (P_(rs_final, 3, 2), P_(deliver, 3))))
    chol(2, ((), (), (), ()))
    chol(3, ((), (), (), ()))
    ag_final(1, 4)

    trail = jnp.logical_and(ci > 0, cj > 0)

    @pl.when(ci > 0)
    def _():
        solve(0, ci)

    @pl.when(trail)
    def _():
        solve(1, cj)

        @pl.loop(0, 2)
        def _(c):
            rows = pl.ds(pl.multiple_of(c * 256, 256), 256)
            out_ref[rows, :] = parent_ref[rows, :] - mm_nt(p_buf[0, rows, :], p_buf[1])
        done = t_buf.at[pl.ds(0, 480)]
        pltpu.make_async_copy(done, done, dist_recv.at[0]).wait()

    @pl.when(jnp.logical_and(trail, ci >= cj))
    def _():
        out_ref[...] = out_ref[...] - t_buf[...]

    @pl.when(jnp.logical_and(trail, ci < cj))
    def _():
        for b in range(4):
            o = b * BLK
            out_ref[:, o:o + BLK] = out_ref[:, o:o + BLK] - t_buf[o:o + BLK, :].T

    @pl.when(jnp.logical_and(ci > 0, cj == 0))
    def _():
        out_ref[...] = p_buf[0]

    @pl.when(jnp.logical_and(ci == 0, cj == 0))
    def _():
        out_ref[...] = ch[...]

    @pl.when(jnp.logical_and(ci == 0, cj > 0))
    def _():
        for c in range(2):
            for a in range(2):
                o = c * 256 + a * 128
                v = jnp.reshape(w_buf[c, 2 * a:2 * a + 2, pl.ds(cj, 1)], (BLK, TILE))
                out_ref[:, o:o + BLK] = -(v.T)

    for cp in started:
        cp.wait_send()
    for mine, cp in deliveries:
        @pl.when(jnp.logical_not(mine))
        def _():
            cp.wait_send()


def body(child_inverse, child_coupling, child_blocks, child_map, parent_front):
    ids = jnp.arange(16)[:, None]
    slots = jnp.arange(8)[None, :]
    hit = jnp.logical_and(child_map[0][None, :] == ids, slots < child_blocks[0])
    slot = jnp.concatenate([jnp.sum(jnp.where(hit, slots, 0), axis=1), jnp.any(hit, axis=1).astype(jnp.int32)]).astype(jnp.int32)
    vm = pltpu.VMEM
    dma = pltpu.SemaphoreType.DMA
    return pl.pallas_call(
        kernel,
        out_shape=jax.ShapeDtypeStruct((TILE, TILE), F32),
        in_specs=[pl.BlockSpec(memory_space=pltpu.SMEM)] + [pl.BlockSpec(memory_space=vm)] * 3,
        out_specs=pl.BlockSpec(memory_space=vm),
        scratch_shapes=[
            vm((8, BLK, TILE), BF16), vm((8, BLK, TILE), BF16),
            vm((2048, TILE), BF16), vm((2048, TILE), BF16),
            vm((2, 4, NT, 64, TILE), F32),
            vm((2, 2, NT, 32, TILE), F32), vm((2, 2, NT, 64, TILE), F32),
            vm((2, 2, NT, 8, TILE), F32), vm((2, 2, NT, 16, TILE), F32),
            vm((2, 4, 4, 64, TILE), F32), vm((2, 6, 16, TILE), F32), vm((TILE, TILE), F32),
            vm((TILE, TILE), F32), vm((BLK, 2 * BLK), F32), vm((4, BLK, BLK), F32), vm((2, TILE, TILE), F32),
            dma((4, 2, 2, 10)), dma((4, 2, 2, 10)), dma((6, 2, 2)), dma((1,)),
        ],
        compiler_params=pltpu.CompilerParams(collective_id=0, has_side_effects=True, vmem_limit_bytes=60 * 1024 * 1024),
    )(slot, child_inverse[0], child_coupling[0], parent_front)


def solution(mesh):
    return jax.shard_map(
        body,
        mesh=mesh,
        in_specs=(
            P(("leaf", "prow", "pcol"), None, None),
            P(("leaf", "prow", "pcol"), None, None),
            P(("leaf", "prow", "pcol")),
            P(("leaf", "prow", "pcol"), None),
            P(("leaf", "prow"), "pcol"),
        ),
        out_specs=P(("leaf", "prow"), "pcol"),
        check_vma=False,
    )
```

```python
import functools

import jax
import jax.numpy as jnp
from jax import lax
from jax.experimental import pallas as pl
from jax.experimental.pallas import tpu as pltpu
from jax.sharding import PartitionSpec as P

BLK = 128
TILE = 512
NT = 10
PACK = (384, 256)
DIAG = (0, 4, 7, 9)
OWNERS = ((1, 1), (2, 1), (3, 1), (2, 2), (3, 2), (3, 3))
AXES = ("prow", "pcol")
F32 = jnp.float32
BF16 = jnp.bfloat16
DN_NT = (((1,), (1,)), ((), ()))


def split(x):
    hi = x.astype(BF16)
    return hi, (x - hi.astype(F32)).astype(BF16)


def dot_nt(a, b):
    return lax.dot_general(a, b, DN_NT, preferred_element_type=F32)


def dot3(a, b):
    return dot_nt(a[0], b[0]) + dot_nt(a[0], b[1]) + dot_nt(a[1], b[0])


def mm_nt(a, b):
    return dot3(split(a), split(b))


def kernel(map_ref, blocks_ref, inv_ref, coup_ref, parent_ref, out_ref,
           fac_h, fac_l, fh, fl, s_buf, rl1, rf1, rf2, g1, g2, w0, wr, wc, z_buf, t_buf,
           ch, md, linv, p_buf,
           send_sem, recv_sem, send2_sem, recv2_sem, xs_sem, xr_sem, pa_send, pa_recv, pb_send, pb_recv, dist_send, dist_recv):
    ci = lax.axis_index("prow")
    cj = lax.axis_index("pcol")
    coord = {"prow": ci, "pcol": cj}
    mesh_id = pl.DeviceIdType.MESH

    def nxt(v, k):
        return lax.rem(v + k, 4)

    def width(t, c):
        return PACK[c] if t in DIAG else TILE

    barrier = pltpu.get_barrier_semaphore()
    for dx in range(4):
        for dy in range(4):
            if dx or dy:
                pl.semaphore_signal(
                    barrier, inc=1,
                    device_id={"prow": nxt(ci, dx), "pcol": nxt(cj, dy)},
                    device_id_type=mesh_id)

    ih, il = split(inv_ref[...])

    @pl.loop(0, 8)
    def _(s):
        c = split(coup_ref[pl.ds(pl.multiple_of(s * BLK, BLK), BLK), :])
        f = dot3(c, (ih, il))
        h, l = split(f)
        fac_h[s] = h
        fac_l[s] = l

    def place(b):
        s = jnp.int32(0)
        found = jnp.int32(0)
        for k in range(8):
            hit = jnp.logical_and(map_ref[0, k] == b, blocks_ref[0] > k)
            s = jnp.where(hit, k, s)
            found = jnp.where(hit, 1, found)
        h = fac_h[s]
        l = fac_l[s]
        rows = pl.ds(pl.multiple_of(b * BLK, BLK), BLK)
        fh[rows, :] = jnp.where(found > 0, h, jnp.zeros_like(h))
        fl[rows, :] = jnp.where(found > 0, l, jnp.zeros_like(l))

    pl.loop(0, 4)(place)

    def tiles(col, lo, hi, base):
        @pl.loop(lo, hi)
        def _(r):
            rows = pl.ds(pl.multiple_of(r * TILE, TILE), TILE)
            cols = pl.ds(col * TILE, TILE)
            d = dot3((fh[rows, :], fl[rows, :]), (fh[cols, :], fl[cols, :]))
            if col == 0:
                mine = jnp.logical_and(ci == r, cj == 0)
                d = d - jnp.where(mine, parent_ref[...], jnp.zeros((TILE, TILE), F32))
            for c in range(2):
                for a in range(4):
                    o = c * 256 + a * 64
                    s_buf[c, a, base + r] = d[o:o + 64]
        if lo == col:
            t = base + col
            for a in range(2):
                s_buf[0, a, t, :, 256:384] = s_buf[1, a, t, :, 256:384]
                s_buf[0, a, t, :, 128:256] = s_buf[1, 2 + a, t, :, 384:512]
                s_buf[0, 2 + a, t, :, 256:384] = s_buf[1, 2 + a, t, :, 256:384]

    def remote(src, dst, ss, rs_, dev):
        return functools.partial(
            pltpu.make_async_remote_copy, src_ref=src, dst_ref=dst, send_sem=ss, recv_sem=rs_,
            device_id=dev, device_id_type=mesh_id)

    started = []

    def go(cp):
        cp().start()
        started.append(cp)

    STEP = (1, 3)

    def x_copy(stage, c, k, src, dst, axis):
        return remote(src, dst, xs_sem.at[stage, c, k - 1], xr_sem.at[stage, c, k - 1], {axis: nxt(coord[axis], k)})

    def x_list(stage):
        out = []
        for k in (2, 1, 3):
            for c in range(2):
                cols = pl.ds(0, PACK[c])
                m, n = coord[AXES[c]], coord[AXES[1 - c]]
                if stage == 0:
                    out.append(x_copy(0, c, k, s_buf.at[c, nxt(m, k), 0, :, cols], g1.at[c, k - 1, :, cols], AXES[c]))
                elif stage == 1:
                    rows = pl.ds(pl.multiple_of(nxt(n, k) * 16, 16), 16)
                    out.append(x_copy(1, c, k, s_buf.at[c, m, 0, rows, cols], g2.at[c, k - 1, :, cols], AXES[1 - c]))
                else:
                    if stage == 2:
                        ref, axis = w0.at[c, m, pl.ds(pl.multiple_of(n * 16, 16), 16), cols], AXES[1 - c]
                    else:
                        ref, axis = w0.at[c, m, :, cols], AXES[c]
                    out.append(x_copy(stage, c, k, ref, ref, axis))
        return out

    def x_start(stage):
        for cp in x_list(stage):
            go(cp)

    def x_wait(stage):
        for cp in x_list(stage):
            cp().wait_recv()
        for c in range(2):
            m, n = coord[AXES[c]], coord[AXES[1 - c]]
            w = PACK[c]
            if stage == 0:
                s_buf[c, m, 0, :, 0:w] = ((s_buf[c, m, 0, :, 0:w] + g1[c, 0, :, 0:w])
                                          + (g1[c, 1, :, 0:w] + g1[c, 2, :, 0:w]))
            elif stage == 1:
                rows = pl.ds(pl.multiple_of(n * 16, 16), 16)
                w0[c, m, rows, 0:w] = ((s_buf[c, m, 0, rows, 0:w] + g2[c, 0, :, 0:w])
                                       + (g2[c, 1, :, 0:w] + g2[c, 2, :, 0:w]))

    def rs(t, c):
        cols = pl.ds(0, width(t, c))
        axis = AXES[c]
        me = coord[axis]

        def chunk(d, h):
            return s_buf.at[c, d, t, pl.ds(h * 32, 32), cols]

        def mk(kind, src, dst, d):
            return remote(src, dst, send_sem.at[t - 1, c, d, kind], recv_sem.at[t - 1, c, d, kind],
                          {axis: nxt(me, STEP[d])})
        relay = [mk(0, chunk(nxt(me, 2), 1 - d), rl1.at[c, d, t, :, cols], d) for d in range(2)]
        raw = [mk(1, chunk(nxt(me, STEP[d]), d), rf1.at[c, d, t, pl.ds(d * 32, 32), cols], d) for d in range(2)]
        fin = [mk(2, chunk(nxt(me, STEP[d]), 1 - d), rf1.at[c, d, t, pl.ds((1 - d) * 32, 32), cols], d)
               for d in range(2)]
        return relay, raw, fin, chunk, me

    def second(t):
        out = []
        for k in (2, 1, 3):
            for c in range(2):
                cols = pl.ds(0, width(t, c))
                m, n = coord[AXES[c]], coord[AXES[1 - c]]
                rows = pl.ds(pl.multiple_of(nxt(n, k) * 16, 16), 16)
                out.append(remote(s_buf.at[c, m, t, rows, cols], rf2.at[c, k - 1, t, :, cols],
                                  send2_sem.at[t - 1, c, k - 1], recv2_sem.at[t - 1, c, k - 1],
                                  {AXES[1 - c]: nxt(n, k)}))
        return out

    def ev_a(t):
        for c in range(2):
            relay, raw = rs(t, c)[:2]
            for d in range(2):
                go(relay[d])
            for d in range(2):
                go(raw[d])

    def ev_b(t):
        for c in range(2):
            relay, raw, fin, chunk, me = rs(t, c)
            for d in range(2):
                relay[d]().wait_recv()
                ref = chunk(nxt(me, STEP[d]), 1 - d)
                ref[...] = ref[...] + rl1[c, d, t, :, 0:width(t, c)]
                go(fin[d])

    def ev_c(t):
        for c in range(2):
            w = width(t, c)
            relay, raw, fin, chunk, me = rs(t, c)
            for d in range(2):
                raw[d]().wait_recv()
                fin[d]().wait_recv()
            m = coord[AXES[c]]
            s_buf[c, m, t, :, 0:w] = s_buf[c, m, t, :, 0:w] + rf1[c, 0, t, :, 0:w] + rf1[c, 1, t, :, 0:w]
        for cp in second(t):
            go(cp)

    def ev_e(t):
        for cp in second(t):
            cp().wait_recv()
        for c in range(2):
            w = width(t, c)
            m, n = coord[AXES[c]], coord[AXES[1 - c]]
            rows = pl.ds(pl.multiple_of(n * 16, 16), 16)
            z_buf[c, t - 1, :, 0:w] = ((s_buf[c, m, t, rows, 0:w] + rf2[c, 0, t, :, 0:w])
                                       + (rf2[c, 1, t, :, 0:w] + rf2[c, 2, t, :, 0:w]))
        if t < 4:
            panel_send(t)
        else:
            deliver(t)

    guarded = []

    def go_unless(mine, cp):
        @pl.when(jnp.logical_not(mine))
        def _():
            cp().start()
        guarded.append((jnp.logical_not(mine), cp))

    def panel_send(t):
        for c in range(2):
            m, n = coord[AXES[c]], coord[AXES[1 - c]]
            rows = pl.ds(pl.multiple_of(n * 16, 16), 16)
            for k, (buf, axis) in enumerate(((wr, "prow"), (wc, "pcol"))):
                mine = coord[axis] == t

                @pl.when(mine)
                def _():
                    buf[c, m, rows, :] = z_buf[c, t - 1]
                go_unless(mine, remote(z_buf.at[c, t - 1], buf.at[c, m, rows], pa_send.at[t - 1, c, k], pa_recv.at[k], {axis: t}))

    def ring(k):
        buf, axis = ((wr, "pcol"), (wc, "prow"))[k]
        me = coord[axis]

        def part(v, c, h, n):
            if c != k:
                return buf.at[c, v, pl.ds(h * 32, n * 32)]
            return buf.at[c, pl.ds(h * 2, n * 2), pl.ds(pl.multiple_of(v * 16, 16), 16)]
        res = []
        for c in range(2):
            for d in range(2):
                def mk(kind, ref):
                    return remote(ref, ref, pb_send.at[k, c, d, kind], pb_recv.at[k, c, d, kind], {axis: nxt(me, STEP[d])})
                prev = nxt(me, STEP[1 - d])
                res.append((mk(0, part(me, c, 0, 2)), mk(0, part(prev, c, 0, 2)),
                            mk(1, part(prev, c, d, 1)), mk(1, part(nxt(me, 2), c, d, 1))))
        return res

    def panel_stage(stage):
        for k in range(2):
            @pl.when((ci, cj)[k] > 0)
            def _():
                if stage == 0:
                    got = (wr, wc)[k].at[0, pl.ds(0, 3), pl.ds(0, 32)]
                    pltpu.make_async_copy(got, got, pa_recv.at[k]).wait()
                for own, own_in, fwd, fwd_in in ring(k):
                    if stage == 0:
                        own().start()
                    elif stage == 1:
                        own_in().wait_recv()
                        fwd().start()
                    elif stage == 2:
                        fwd_in().wait_recv()
                    else:
                        own().wait_send()
                        fwd().wait_send()

    def deliver(t):
        r, q = OWNERS[t - 4]
        for k, (x, y) in enumerate(((r, q), (q, r))[: 1 if r == q else 2]):
            mine = jnp.logical_and(ci == x, cj == y)
            for c in range(2):
                cols = pl.ds(0, width(t, c))
                m, v = coord[AXES[c]], coord[AXES[1 - c]]
                rows = pl.ds(pl.multiple_of(c * 256 + m * 64 + v * 16, 16), 16)

                @pl.when(mine)
                def _():
                    t_buf[rows, cols] = z_buf[c, t - 1, :, cols]
                go_unless(mine, remote(z_buf.at[c, t - 1, :, cols], t_buf.at[rows, cols], dist_send.at[t - 4, k, c],
                                       dist_recv.at[0], {"prow": x, "pcol": y}))

    def chol_begin(kb):
        o = kb * BLK
        eye = lax.broadcasted_iota(jnp.int32, (BLK, BLK), 0) == lax.broadcasted_iota(jnp.int32, (BLK, BLK), 1)
        md[:, 0:BLK] = ch[o:o + BLK, o:o + BLK]
        md[:, BLK:2 * BLK] = eye.astype(F32)

    def chol_chunk(q):
        lo = q * 32
        x = md[lo:BLK, 0:BLK]
        y = md[lo:BLK, BLK:2 * BLK]
        rid = lax.broadcasted_iota(jnp.int32, (BLK - lo, BLK), 0)
        for k in range(0, 32, 2):
            c0 = jnp.broadcast_to(x[:, lo + k:lo + k + 1], x.shape)
            c1 = jnp.broadcast_to(x[:, lo + k + 1:lo + k + 2], x.shape)
            a = c0[k:k + 1, :]
            b = c0[k + 1:k + 2, :]
            d = c1[k + 1:k + 2, :]
            ia = 1.0 / a
            ba = b * ia
            s = d - b * ba
            isv = 1.0 / s
            m0 = jnp.where(rid > k + 1, c0, 0.0)
            m1 = jnp.where(rid > k + 1, c1, 0.0) - m0 * ba
            m0 = jnp.where(rid == k + 1, b, m0)
            xa = x[k:k + 1, :]
            ya = y[k:k + 1, :]
            xb = (x[k + 1:k + 2, :] - ba * xa) * isv
            yb = (y[k + 1:k + 2, :] - ba * ya) * isv
            xa = xa * ia
            ya = ya * ia
            x = x - m0 * xa - m1 * xb
            y = y - m0 * ya - m1 * yb
        md[lo:BLK, 0:BLK] = x
        md[lo:BLK, BLK:2 * BLK] = y

    def chol_end(kb):
        o = kb * BLK
        ri = lax.broadcasted_iota(jnp.int32, (BLK, BLK), 0)
        cj_ = lax.broadcasted_iota(jnp.int32, (BLK, BLK), 1)
        u = md[:, 0:BLK]
        piv = jnp.sum(jnp.where(ri == cj_, u, 0.0), axis=1, keepdims=True)
        sc = lax.rsqrt(piv)
        li = md[:, BLK:2 * BLK] * sc
        linv[kb] = li
        low = jnp.where(cj_ >= ri, u * sc, 0.0).T
        ch[o:o + BLK, o:o + BLK] = low
        if kb < 3:
            lp = lax.dot_general(ch[o + BLK:, o:o + BLK], li, DN_NT, precision=lax.Precision.HIGHEST,
                                 preferred_element_type=F32)
            ch[o + BLK:, o:o + BLK] = lp
            ch[o + BLK:, o + BLK:] = ch[o + BLK:, o + BLK:] - lax.dot_general(
                lp, lp, DN_NT, precision=lax.Precision.HIGHEST, preferred_element_type=F32)
            ch[o:o + BLK, o + BLK:] = jnp.zeros((BLK, TILE - o - BLK), F32)

    def solve(x, buf):
        @pl.loop(0, 2)
        def _(c):
            a = -jnp.reshape(buf[c], (256, TILE))
            rows = pl.ds(pl.multiple_of(c * 256, 256), 256)
            for b in range(4):
                o = b * BLK
                v = a[:, o:o + BLK]
                if b:
                    v = v - mm_nt(p_buf[x, rows, 0:o], ch[o:o + BLK, 0:o])
                p_buf[x, rows, o:o + BLK] = mm_nt(v, linv[b])

    tiles(0, 0, 1, 0)
    pl.semaphore_wait(barrier, 15)
    x_start(0)
    pl.loop(4, 16)(place)
    tiles(0, 1, 4, 0)
    ev_a(1)
    x_wait(0)
    x_start(1)
    ev_a(2)
    tiles(1, 1, 4, 3)
    x_wait(1)
    x_start(2)
    ev_b(1)
    ev_a(3)
    x_wait(2)
    x_start(3)
    ev_b(2)
    ev_a(4)
    tiles(2, 2, 4, 5)
    tiles(3, 3, 4, 6)
    ev_c(1)

    fn = {"a": ev_a, "b": ev_b, "c": ev_c, "e": ev_e, "p": panel_stage}
    order = ("b3 a5 c2", "e1 b4 a6", "c3 e2 b5", "a7 c4 e3", "b6 a8 c5", "p0 e4 b7", "a9 c6 p1", "e5 b8 c7",
             "p2 e6 b9", "c8 e7 c9", "e8 e9")
    order = [w for part in order for w in part.split()]
    head = 28
    x_wait(3)
    ch[...] = jnp.zeros((TILE, TILE), F32)
    for a in range(4):
        o = a * 64
        n = 128 * (1 + a // 2)
        ch[o:o + 64, 0:n] = -w0[0, a, :, 0:n]
        ch[256 + o:320 + o, 0:256] = -w0[1, a, :, 0:256]
        ch[256 + o:320 + o, 256:384] = -w0[0, a, :, 256:384]
    for a in range(2):
        ch[384 + a * 64:448 + a * 64, 384:512] = -w0[0, a, :, 128:256]

    at = 0
    for kb in range(4):
        chol_begin(kb)
        for q in range(4):
            upto = (head * (4 * kb + q + 1)) // 16
            while at < upto:
                fn[order[at][0]](int(order[at][1]))
                at += 1
            chol_chunk(q)
        chol_end(kb)

    trail = jnp.logical_and(ci > 0, cj > 0)
    for n, w in enumerate(order[head:]):
        fn[w[0]](int(w[1]))
        if n == 1:
            @pl.when(ci > 0)
            def _():
                solve(0, wr)
        if n == 3:
            @pl.when(trail)
            def _():
                solve(1, wc)

                @pl.loop(0, 2)
                def _(c):
                    rows = pl.ds(pl.multiple_of(c * 256, 256), 256)
                    out_ref[rows, :] = parent_ref[rows, :] - mm_nt(p_buf[0, rows, :], p_buf[1])

    def arrived(rows, w):
        done = t_buf.at[pl.ds(0, rows), pl.ds(0, w)]
        pltpu.make_async_copy(done, done, dist_recv.at[0]).wait()

    @pl.when(jnp.logical_and(trail, ci == cj))
    def _():
        arrived(400, 384)
        for p in range(4):
            for q in range(p + 1):
                y, x = {(2, 2): (0, 2), (3, 2): (1, 2), (3, 3): (0, 1)}.get((p, q), (p, q))
                v = t_buf[y * BLK:(y + 1) * BLK, x * BLK:(x + 1) * BLK]
                out_ref[p * BLK:(p + 1) * BLK, q * BLK:(q + 1) * BLK] -= v
                if p != q:
                    out_ref[q * BLK:(q + 1) * BLK, p * BLK:(p + 1) * BLK] -= v.T

    @pl.when(jnp.logical_and(trail, ci > cj))
    def _():
        arrived(480, TILE)
        out_ref[...] = out_ref[...] - t_buf[...]

    @pl.when(jnp.logical_and(trail, ci < cj))
    def _():
        arrived(480, TILE)
        for b in range(4):
            o = b * BLK
            out_ref[:, o:o + BLK] = out_ref[:, o:o + BLK] - t_buf[o:o + BLK, :].T

    @pl.when(jnp.logical_and(ci > 0, cj == 0))
    def _():
        out_ref[...] = p_buf[0]

    @pl.when(jnp.logical_and(ci == 0, cj == 0))
    def _():
        out_ref[...] = ch[...]

    @pl.when(jnp.logical_and(ci == 0, cj > 0))
    def _():
        for c in range(2):
            for a in range(2):
                o = c * 256 + a * 128
                out_ref[:, o:o + BLK] = -(jnp.reshape(wc[c, 2 * a:2 * a + 2], (BLK, TILE)).T)

    for cp in started:
        cp().wait_send()
    panel_stage(3)
    for cond, cp in guarded:
        @pl.when(cond)
        def _():
            cp().wait_send()


def body(child_inverse, child_coupling, child_blocks, child_map, parent_front):
    vm = pltpu.VMEM
    dma = pltpu.SemaphoreType.DMA
    return pl.pallas_call(
        kernel,
        out_shape=jax.ShapeDtypeStruct((TILE, TILE), F32),
        in_specs=[pl.BlockSpec(memory_space=pltpu.SMEM)] * 2 + [pl.BlockSpec(memory_space=vm)] * 3,
        out_specs=pl.BlockSpec(memory_space=vm),
        scratch_shapes=[
            vm((8, BLK, TILE), BF16), vm((8, BLK, TILE), BF16),
            vm((2048, TILE), BF16), vm((2048, TILE), BF16),
            vm((2, 4, NT, 64, TILE), F32),
            vm((2, 2, NT, 32, TILE), F32), vm((2, 2, NT, 64, TILE), F32),
            vm((2, 3, NT, 16, TILE), F32),
            vm((2, 3, 64, 384), F32), vm((2, 3, 16, 384), F32), vm((2, 4, 64, 384), F32),
            vm((2, 4, 64, TILE), F32), vm((2, 4, 64, TILE), F32),
            vm((2, 9, 16, TILE), F32), vm((TILE, TILE), F32),
            vm((TILE, TILE), F32), vm((BLK, 2 * BLK), F32), vm((4, BLK, BLK), F32), vm((2, TILE, TILE), F32),
            dma((9, 2, 2, 3)), dma((9, 2, 2, 3)), dma((9, 2, 3)), dma((9, 2, 3)), dma((4, 2, 3)), dma((4, 2, 3)),
            dma((3, 2, 2)), dma((2,)), dma((2, 2, 2, 2)), dma((2, 2, 2, 2)), dma((6, 2, 2)), dma((1,)),
        ],
        compiler_params=pltpu.CompilerParams(collective_id=0, has_side_effects=True, vmem_limit_bytes=46 * 1024 * 1024),
    )(child_map, child_blocks, child_inverse[0], child_coupling[0], parent_front)


def solution(mesh):
    return jax.shard_map(
        body,
        mesh=mesh,
        in_specs=(
            P(("leaf", "prow", "pcol"), None, None),
            P(("leaf", "prow", "pcol"), None, None),
            P(("leaf", "prow", "pcol")),
            P(("leaf", "prow", "pcol"), None),
            P(("leaf", "prow"), "pcol"),
        ),
        out_specs=P(("leaf", "prow"), "pcol"),
        check_vma=False,
    )
```

```python
import functools

import jax
import jax.numpy as jnp
from jax import lax
from jax.experimental import pallas as pl
from jax.experimental.pallas import tpu as pltpu
from jax.sharding import PartitionSpec as P

BLK = 128
TILE = 512
NT = 10
PACK = (384, 256)
DIAG = (0, 4, 7, 9)
OWNERS = ((1, 1), (2, 1), (3, 1), (2, 2), (3, 2), (3, 3))
AXES = ("prow", "pcol")
F32 = jnp.float32
BF16 = jnp.bfloat16
DN_NT = (((1,), (1,)), ((), ()))


def split(x):
    hi = x.astype(BF16)
    return hi, (x - hi.astype(F32)).astype(BF16)


def dot_nt(a, b):
    return lax.dot_general(a, b, DN_NT, preferred_element_type=F32)


def dot3(a, b):
    return dot_nt(a[0], b[0]) + dot_nt(a[0], b[1]) + dot_nt(a[1], b[0])


def mm_nt(a, b):
    return dot3(split(a), split(b))


def kernel(map_hbm, blocks_ref, inv_hbm, coup_hbm, parent_hbm, out_ref,
           map_ref, inv_ref, coup_ref, parent_ref, in_sem,
           fac_h, fac_l, fh, fl, s_buf, rl1, rf1, rf2, g1, g2, w0, wr, wc, z_buf, t_buf,
           ch, md, linv, p_buf,
           send_sem, recv_sem, send2_sem, recv2_sem, xs_sem, xr_sem, pa_send, pa_recv, pb_send, pb_recv, dist_send, dist_recv):
    ci = lax.axis_index("prow")
    cj = lax.axis_index("pcol")
    coord = {"prow": ci, "pcol": cj}
    mesh_id = pl.DeviceIdType.MESH

    def nxt(v, k):
        return lax.rem(v + k, 4)

    def width(t, c):
        return PACK[c] if t in DIAG else TILE

    load_inv = pltpu.make_async_copy(inv_hbm, inv_ref, in_sem.at[0])
    load_inv.start()
    load_map = pltpu.make_async_copy(map_hbm, map_ref, in_sem.at[1])
    loads = []
    for s in range(4):
        rows = pl.ds(s * 256, 256)
        loads.append(pltpu.make_async_copy(coup_hbm.at[rows], coup_ref.at[rows], in_sem.at[3 + s]))
        loads[s].start()
    load_map.start()
    load_parent = pltpu.make_async_copy(parent_hbm, parent_ref, in_sem.at[2])
    load_parent.start()

    barrier = pltpu.get_barrier_semaphore()
    for dx in range(4):
        for dy in range(4):
            if dx or dy:
                pl.semaphore_signal(
                    barrier, inc=1,
                    device_id={"prow": nxt(ci, dx), "pcol": nxt(cj, dy)},
                    device_id_type=mesh_id)

    load_inv.wait()
    ih, il = split(inv_ref[...])
    for s in range(4):
        loads[s].wait()
        c = split(coup_ref[s * 256:s * 256 + 256, :])
        h, l = split(dot3(c, (ih, il)))
        for k in range(2):
            fac_h[2 * s + k] = h[k * BLK:k * BLK + BLK]
            fac_l[2 * s + k] = l[k * BLK:k * BLK + BLK]
    load_map.wait()
    load_parent.wait()

    def place(b):
        s = jnp.int32(0)
        found = jnp.int32(0)
        for k in range(8):
            hit = jnp.logical_and(map_ref[0, k] == b, blocks_ref[0] > k)
            s = jnp.where(hit, k, s)
            found = jnp.where(hit, 1, found)
        h = fac_h[s]
        l = fac_l[s]
        rows = pl.ds(pl.multiple_of(b * BLK, BLK), BLK)
        fh[rows, :] = jnp.where(found > 0, h, jnp.zeros_like(h))
        fl[rows, :] = jnp.where(found > 0, l, jnp.zeros_like(l))

    pl.loop(0, 4)(place)

    def tiles(col, lo, hi, base):
        @pl.loop(lo, hi)
        def _(r):
            rows = pl.ds(pl.multiple_of(r * TILE, TILE), TILE)
            cols = pl.ds(col * TILE, TILE)
            d = dot3((fh[rows, :], fl[rows, :]), (fh[cols, :], fl[cols, :]))
            if col == 0:
                mine = jnp.logical_and(ci == r, cj == 0)
                d = d - jnp.where(mine, parent_ref[...], jnp.zeros((TILE, TILE), F32))
            for c in range(2):
                for a in range(4):
                    o = c * 256 + a * 64
                    s_buf[c, a, base + r] = d[o:o + 64]
        if lo == col:
            t = base + col
            for a in range(2):
                s_buf[0, a, t, :, 256:384] = s_buf[1, a, t, :, 256:384]
                s_buf[0, a, t, :, 128:256] = s_buf[1, 2 + a, t, :, 384:512]
                s_buf[0, 2 + a, t, :, 256:384] = s_buf[1, 2 + a, t, :, 256:384]

    def remote(src, dst, ss, rs_, dev):
        return functools.partial(
            pltpu.make_async_remote_copy, src_ref=src, dst_ref=dst, send_sem=ss, recv_sem=rs_,
            device_id=dev, device_id_type=mesh_id)

    started = []

    def go(cp):
        cp().start()
        started.append(cp)

    STEP = (1, 3)

    def x_copy(stage, c, k, src, dst, axis):
        return remote(src, dst, xs_sem.at[stage, c, k - 1], xr_sem.at[stage, c, k - 1], {axis: nxt(coord[axis], k)})

    def x_list(stage):
        out = []
        for k in (2, 1, 3):
            for c in range(2):
                cols = pl.ds(0, PACK[c])
                m, n = coord[AXES[c]], coord[AXES[1 - c]]
                if stage == 0:
                    out.append(x_copy(0, c, k, s_buf.at[c, nxt(m, k), 0, :, cols], g1.at[c, k - 1, :, cols], AXES[c]))
                elif stage == 1:
                    rows = pl.ds(pl.multiple_of(nxt(n, k) * 16, 16), 16)
                    out.append(x_copy(1, c, k, s_buf.at[c, m, 0, rows, cols], g2.at[c, k - 1, :, cols], AXES[1 - c]))
                else:
                    if stage == 2:
                        ref, axis = w0.at[c, m, pl.ds(pl.multiple_of(n * 16, 16), 16), cols], AXES[1 - c]
                    else:
                        ref, axis = w0.at[c, m, :, cols], AXES[c]
                    out.append(x_copy(stage, c, k, ref, ref, axis))
        return out

    def x_start(stage):
        for cp in x_list(stage):
            go(cp)

    def x_wait(stage):
        for cp in x_list(stage):
            cp().wait_recv()
        for c in range(2):
            m, n = coord[AXES[c]], coord[AXES[1 - c]]
            w = PACK[c]
            if stage == 0:
                s_buf[c, m, 0, :, 0:w] = ((s_buf[c, m, 0, :, 0:w] + g1[c, 0, :, 0:w])
                                          + (g1[c, 1, :, 0:w] + g1[c, 2, :, 0:w]))
            elif stage == 1:
                rows = pl.ds(pl.multiple_of(n * 16, 16), 16)
                w0[c, m, rows, 0:w] = ((s_buf[c, m, 0, rows, 0:w] + g2[c, 0, :, 0:w])
                                       + (g2[c, 1, :, 0:w] + g2[c, 2, :, 0:w]))

    def rs(t, c):
        cols = pl.ds(0, width(t, c))
        axis = AXES[c]
        me = coord[axis]

        def chunk(d, h):
            return s_buf.at[c, d, t, pl.ds(h * 32, 32), cols]

        def mk(kind, src, dst, d):
            return remote(src, dst, send_sem.at[t - 1, c, d, kind], recv_sem.at[t - 1, c, d, kind],
                          {axis: nxt(me, STEP[d])})
        relay = [mk(0, chunk(nxt(me, 2), 1 - d), rl1.at[c, d, t, :, cols], d) for d in range(2)]
        raw = [mk(1, chunk(nxt(me, STEP[d]), d), rf1.at[c, d, t, pl.ds(d * 32, 32), cols], d) for d in range(2)]
        fin = [mk(2, chunk(nxt(me, STEP[d]), 1 - d), rf1.at[c, d, t, pl.ds((1 - d) * 32, 32), cols], d)
               for d in range(2)]
        return relay, raw, fin, chunk, me

    def second(t):
        out = []
        for k in (2, 1, 3):
            for c in range(2):
                cols = pl.ds(0, width(t, c))
                m, n = coord[AXES[c]], coord[AXES[1 - c]]
                rows = pl.ds(pl.multiple_of(nxt(n, k) * 16, 16), 16)
                out.append(remote(s_buf.at[c, m, t, rows, cols], rf2.at[c, k - 1, t, :, cols],
                                  send2_sem.at[t - 1, c, k - 1], recv2_sem.at[t - 1, c, k - 1],
                                  {AXES[1 - c]: nxt(n, k)}))
        return out

    def ev_a(t):
        for c in range(2):
            relay, raw = rs(t, c)[:2]
            for d in range(2):
                go(relay[d])
            for d in range(2):
                go(raw[d])

    def ev_b(t):
        for c in range(2):
            relay, raw, fin, chunk, me = rs(t, c)
            for d in range(2):
                relay[d]().wait_recv()
                ref = chunk(nxt(me, STEP[d]), 1 - d)
                ref[...] = ref[...] + rl1[c, d, t, :, 0:width(t, c)]
                go(fin[d])

    def ev_c(t):
        for c in range(2):
            w = width(t, c)
            relay, raw, fin, chunk, me = rs(t, c)
            for d in range(2):
                raw[d]().wait_recv()
                fin[d]().wait_recv()
            m = coord[AXES[c]]
            s_buf[c, m, t, :, 0:w] = s_buf[c, m, t, :, 0:w] + rf1[c, 0, t, :, 0:w] + rf1[c, 1, t, :, 0:w]
        for cp in second(t):
            go(cp)

    def ev_e(t):
        for cp in second(t):
            cp().wait_recv()
        for c in range(2):
            w = width(t, c)
            m, n = coord[AXES[c]], coord[AXES[1 - c]]
            rows = pl.ds(pl.multiple_of(n * 16, 16), 16)
            z_buf[c, t - 1, :, 0:w] = ((s_buf[c, m, t, rows, 0:w] + rf2[c, 0, t, :, 0:w])
                                       + (rf2[c, 1, t, :, 0:w] + rf2[c, 2, t, :, 0:w]))
        if t < 4:
            panel_send(t)
        else:
            deliver(t)

    guarded = []

    def go_unless(mine, cp):
        @pl.when(jnp.logical_not(mine))
        def _():
            cp().start()
        guarded.append((jnp.logical_not(mine), cp))

    def panel_send(t):
        for c in range(2):
            m, n = coord[AXES[c]], coord[AXES[1 - c]]
            rows = pl.ds(pl.multiple_of(n * 16, 16), 16)
            for k, (buf, axis) in enumerate(((wr, "prow"), (wc, "pcol"))):
                mine = coord[axis] == t

                @pl.when(mine)
                def _():
                    buf[c, m, rows, :] = z_buf[c, t - 1]
                go_unless(mine, remote(z_buf.at[c, t - 1], buf.at[c, m, rows], pa_send.at[t - 1, c, k], pa_recv.at[k], {axis: t}))

    def ring(k):
        buf, axis = ((wr, "pcol"), (wc, "prow"))[k]
        me = coord[axis]

        def part(v, c, h, n):
            if c != k:
                return buf.at[c, v, pl.ds(h * 32, n * 32)]
            return buf.at[c, pl.ds(h * 2, n * 2), pl.ds(pl.multiple_of(v * 16, 16), 16)]
        res = []
        for c in range(2):
            for d in range(2):
                def mk(kind, ref):
                    return remote(ref, ref, pb_send.at[k, c, d, kind], pb_recv.at[k, c, d, kind], {axis: nxt(me, STEP[d])})
                prev = nxt(me, STEP[1 - d])
                res.append((mk(0, part(me, c, 0, 2)), mk(0, part(prev, c, 0, 2)),
                            mk(1, part(prev, c, d, 1)), mk(1, part(nxt(me, 2), c, d, 1))))
        return res

    def panel_stage(stage):
        for k in range(2):
            @pl.when((ci, cj)[k] > 0)
            def _():
                if stage == 0:
                    got = (wr, wc)[k].at[0, pl.ds(0, 3), pl.ds(0, 32)]
                    pltpu.make_async_copy(got, got, pa_recv.at[k]).wait()
                for own, own_in, fwd, fwd_in in ring(k):
                    if stage == 0:
                        own().start()
                    elif stage == 1:
                        own_in().wait_recv()
                        fwd().start()
                    elif stage == 2:
                        fwd_in().wait_recv()
                    else:
                        own().wait_send()
                        fwd().wait_send()

    def deliver(t):
        r, q = OWNERS[t - 4]
        for k, (x, y) in enumerate(((r, q), (q, r))[: 1 if r == q else 2]):
            mine = jnp.logical_and(ci == x, cj == y)
            for c in range(2):
                cols = pl.ds(0, width(t, c))
                m, v = coord[AXES[c]], coord[AXES[1 - c]]
                rows = pl.ds(pl.multiple_of(c * 256 + m * 64 + v * 16, 16), 16)

                @pl.when(mine)
                def _():
                    t_buf[rows, cols] = z_buf[c, t - 1, :, cols]
                go_unless(mine, remote(z_buf.at[c, t - 1, :, cols], t_buf.at[rows, cols], dist_send.at[t - 4, k, c],
                                       dist_recv.at[0], {"prow": x, "pcol": y}))

    def chol_begin(kb):
        o = kb * BLK
        eye = lax.broadcasted_iota(jnp.int32, (BLK, BLK), 0) == lax.broadcasted_iota(jnp.int32, (BLK, BLK), 1)
        md[:, 0:BLK] = ch[o:o + BLK, o:o + BLK]
        md[:, BLK:2 * BLK] = eye.astype(F32)

    def chol_chunk(q):
        lo = q * 32
        x = md[lo:BLK, 0:BLK]
        y = md[lo:BLK, BLK:2 * BLK]
        rid = lax.broadcasted_iota(jnp.int32, (BLK - lo, BLK), 0)
        for k in range(0, 32, 2):
            c0 = jnp.broadcast_to(x[:, lo + k:lo + k + 1], x.shape)
            c1 = jnp.broadcast_to(x[:, lo + k + 1:lo + k + 2], x.shape)
            a = c0[k:k + 1, :]
            b = c0[k + 1:k + 2, :]
            d = c1[k + 1:k + 2, :]
            ia = 1.0 / a
            ba = b * ia
            s = d - b * ba
            isv = 1.0 / s
            m0 = jnp.where(rid > k + 1, c0, 0.0)
            m1 = jnp.where(rid > k + 1, c1, 0.0) - m0 * ba
            m0 = jnp.where(rid == k + 1, b, m0)
            xa = x[k:k + 1, :]
            ya = y[k:k + 1, :]
            xb = (x[k + 1:k + 2, :] - ba * xa) * isv
            yb = (y[k + 1:k + 2, :] - ba * ya) * isv
            xa = xa * ia
            ya = ya * ia
            x = x - m0 * xa - m1 * xb
            y = y - m0 * ya - m1 * yb
        md[lo:BLK, 0:BLK] = x
        md[lo:BLK, BLK:2 * BLK] = y

    def chol_end(kb):
        o = kb * BLK
        ri = lax.broadcasted_iota(jnp.int32, (BLK, BLK), 0)
        cj_ = lax.broadcasted_iota(jnp.int32, (BLK, BLK), 1)
        u = md[:, 0:BLK]
        piv = jnp.sum(jnp.where(ri == cj_, u, 0.0), axis=1, keepdims=True)
        sc = lax.rsqrt(piv)
        li = md[:, BLK:2 * BLK] * sc
        linv[kb] = li
        low = jnp.where(cj_ >= ri, u * sc, 0.0).T
        ch[o:o + BLK, o:o + BLK] = low
        if kb < 3:
            lp = lax.dot_general(ch[o + BLK:, o:o + BLK], li, DN_NT, precision=lax.Precision.HIGHEST,
                                 preferred_element_type=F32)
            ch[o + BLK:, o:o + BLK] = lp
            ch[o + BLK:, o + BLK:] = ch[o + BLK:, o + BLK:] - lax.dot_general(
                lp, lp, DN_NT, precision=lax.Precision.HIGHEST, preferred_element_type=F32)
            ch[o:o + BLK, o + BLK:] = jnp.zeros((BLK, TILE - o - BLK), F32)

    def solve(x, buf):
        @pl.loop(0, 2)
        def _(c):
            a = -jnp.reshape(buf[c], (256, TILE))
            rows = pl.ds(pl.multiple_of(c * 256, 256), 256)
            for b in range(4):
                o = b * BLK
                v = a[:, o:o + BLK]
                if b:
                    v = v - mm_nt(p_buf[x, rows, 0:o], ch[o:o + BLK, 0:o])
                p_buf[x, rows, o:o + BLK] = mm_nt(v, linv[b])

    tiles(0, 0, 1, 0)
    pl.semaphore_wait(barrier, 15)
    x_start(0)
    pl.loop(4, 16)(place)
    tiles(0, 1, 4, 0)
    ev_a(1)
    x_wait(0)
    x_start(1)
    ev_a(2)
    tiles(1, 1, 4, 3)
    x_wait(1)
    x_start(2)
    ev_b(1)
    ev_a(3)
    x_wait(2)
    x_start(3)
    ev_b(2)
    ev_a(4)
    tiles(2, 2, 4, 5)
    tiles(3, 3, 4, 6)
    ev_c(1)

    fn = {"a": ev_a, "b": ev_b, "c": ev_c, "e": ev_e, "p": panel_stage}
    order = ("b3 a5 c2", "e1 b4 a6", "c3 e2 b5", "a7 c4 e3", "b6 a8 c5", "p0 e4 b7", "a9 c6 p1", "e5 b8 c7",
             "p2 e6 b9", "c8 e7 c9", "e8 e9")
    order = [w for part in order for w in part.split()]
    head = 28
    x_wait(3)
    ch[...] = jnp.zeros((TILE, TILE), F32)
    for a in range(4):
        o = a * 64
        n = 128 * (1 + a // 2)
        ch[o:o + 64, 0:n] = -w0[0, a, :, 0:n]
        ch[256 + o:320 + o, 0:256] = -w0[1, a, :, 0:256]
        ch[256 + o:320 + o, 256:384] = -w0[0, a, :, 256:384]
    for a in range(2):
        ch[384 + a * 64:448 + a * 64, 384:512] = -w0[0, a, :, 128:256]

    at = 0
    for kb in range(4):
        chol_begin(kb)
        for q in range(4):
            upto = (head * (4 * kb + q + 1)) // 16
            while at < upto:
                fn[order[at][0]](int(order[at][1]))
                at += 1
            chol_chunk(q)
        chol_end(kb)

    trail = jnp.logical_and(ci > 0, cj > 0)
    for n, w in enumerate(order[head:]):
        fn[w[0]](int(w[1]))
        if n == 1:
            @pl.when(ci > 0)
            def _():
                solve(0, wr)
        if n == 3:
            @pl.when(trail)
            def _():
                solve(1, wc)

                @pl.loop(0, 2)
                def _(c):
                    rows = pl.ds(pl.multiple_of(c * 256, 256), 256)
                    out_ref[rows, :] = parent_ref[rows, :] - mm_nt(p_buf[0, rows, :], p_buf[1])

    def arrived(rows, w):
        done = t_buf.at[pl.ds(0, rows), pl.ds(0, w)]
        pltpu.make_async_copy(done, done, dist_recv.at[0]).wait()

    @pl.when(jnp.logical_and(trail, ci == cj))
    def _():
        arrived(400, 384)
        for p in range(4):
            for q in range(p + 1):
                y, x = {(2, 2): (0, 2), (3, 2): (1, 2), (3, 3): (0, 1)}.get((p, q), (p, q))
                v = t_buf[y * BLK:(y + 1) * BLK, x * BLK:(x + 1) * BLK]
                out_ref[p * BLK:(p + 1) * BLK, q * BLK:(q + 1) * BLK] -= v
                if p != q:
                    out_ref[q * BLK:(q + 1) * BLK, p * BLK:(p + 1) * BLK] -= v.T

    @pl.when(jnp.logical_and(trail, ci > cj))
    def _():
        arrived(480, TILE)
        out_ref[...] = out_ref[...] - t_buf[...]

    @pl.when(jnp.logical_and(trail, ci < cj))
    def _():
        arrived(480, TILE)
        for b in range(4):
            o = b * BLK
            out_ref[:, o:o + BLK] = out_ref[:, o:o + BLK] - t_buf[o:o + BLK, :].T

    @pl.when(jnp.logical_and(ci > 0, cj == 0))
    def _():
        out_ref[...] = p_buf[0]

    @pl.when(jnp.logical_and(ci == 0, cj == 0))
    def _():
        out_ref[...] = ch[...]

    @pl.when(jnp.logical_and(ci == 0, cj > 0))
    def _():
        for c in range(2):
            for a in range(2):
                o = c * 256 + a * 128
                out_ref[:, o:o + BLK] = -(jnp.reshape(wc[c, 2 * a:2 * a + 2], (BLK, TILE)).T)

    for cp in started:
        cp().wait_send()
    panel_stage(3)
    for cond, cp in guarded:
        @pl.when(cond)
        def _():
            cp().wait_send()


def body(child_inverse, child_coupling, child_blocks, child_map, parent_front):
    vm = pltpu.VMEM
    dma = pltpu.SemaphoreType.DMA
    return pl.pallas_call(
        kernel,
        out_shape=jax.ShapeDtypeStruct((TILE, TILE), F32),
        in_specs=[pl.BlockSpec(memory_space=pltpu.SMEM if k == 1 else pltpu.HBM) for k in range(5)],
        out_specs=pl.BlockSpec(memory_space=vm),
        scratch_shapes=[
            pltpu.SMEM((1, 8), jnp.int32), vm((TILE, TILE), F32), vm((1024, TILE), F32), vm((TILE, TILE), F32), dma((7,)),
            vm((8, BLK, TILE), BF16), vm((8, BLK, TILE), BF16),
            vm((2048, TILE), BF16), vm((2048, TILE), BF16),
            vm((2, 4, NT, 64, TILE), F32),
            vm((2, 2, NT, 32, TILE), F32), vm((2, 2, NT, 64, TILE), F32),
            vm((2, 3, NT, 16, TILE), F32),
            vm((2, 3, 64, 384), F32), vm((2, 3, 16, 384), F32), vm((2, 4, 64, 384), F32),
            vm((2, 4, 64, TILE), F32), vm((2, 4, 64, TILE), F32),
            vm((2, 9, 16, TILE), F32), vm((TILE, TILE), F32),
            vm((TILE, TILE), F32), vm((BLK, 2 * BLK), F32), vm((4, BLK, BLK), F32), vm((2, TILE, TILE), F32),
            dma((9, 2, 2, 3)), dma((9, 2, 2, 3)), dma((9, 2, 3)), dma((9, 2, 3)), dma((4, 2, 3)), dma((4, 2, 3)),
            dma((3, 2, 2)), dma((2,)), dma((2, 2, 2, 2)), dma((2, 2, 2, 2)), dma((6, 2, 2)), dma((1,)),
        ],
        compiler_params=pltpu.CompilerParams(collective_id=0, has_side_effects=True, vmem_limit_bytes=60 * 1024 * 1024),
    )(child_map, child_blocks, child_inverse[0], child_coupling[0], parent_front)


def solution(mesh):
    return jax.shard_map(
        body,
        mesh=mesh,
        in_specs=(
            P(("leaf", "prow", "pcol"), None, None),
            P(("leaf", "prow", "pcol"), None, None),
            P(("leaf", "prow", "pcol")),
            P(("leaf", "prow", "pcol"), None),
            P(("leaf", "prow"), "pcol"),
        ),
        out_specs=P(("leaf", "prow"), "pcol"),
        check_vma=False,
    )
```

```python
import functools

import jax
import jax.numpy as jnp
from jax import lax
from jax.experimental import pallas as pl
from jax.experimental.pallas import tpu as pltpu
from jax.sharding import PartitionSpec as P

BLK = 128
TILE = 512
NT = 10
PACK = (384, 256)
DIAG = (0, 4, 7, 9)
OWNERS = ((1, 1), (2, 1), (3, 1), (2, 2), (3, 2), (3, 3))
AXES = ("prow", "pcol")
F32 = jnp.float32
BF16 = jnp.bfloat16
DN_NT = (((1,), (1,)), ((), ()))


def split(x):
    hi = x.astype(BF16)
    return hi, (x - hi.astype(F32)).astype(BF16)


def dot_nt(a, b):
    return lax.dot_general(a, b, DN_NT, preferred_element_type=F32)


def dot3(a, b):
    return dot_nt(a[0], b[0]) + dot_nt(a[0], b[1]) + dot_nt(a[1], b[0])


def mm_nt(a, b):
    return dot3(split(a), split(b))


def kernel(map_hbm, blocks_ref, inv_hbm, coup_hbm, parent_hbm, out_ref,
           map_ref, inv_ref, coup_ref, parent_ref, in_sem,
           fac_h, fac_l, fh, fl, s_buf, rl1, rf1, rf2, g1, g2, w0, wr, wc, z_buf, t_buf,
           ch, md, linv, p_buf,
           send_sem, recv_sem, send2_sem, recv2_sem, xs_sem, xr_sem, xf_send, xf_recv, pa_send, pa_recv, pb_send, pb_recv, dist_send, dist_recv):
    ci = lax.axis_index("prow")
    cj = lax.axis_index("pcol")
    coord = {"prow": ci, "pcol": cj}
    mesh_id = pl.DeviceIdType.MESH

    def nxt(v, k):
        return lax.rem(v + k, 4)

    def width(t, c):
        return PACK[c] if t in DIAG else TILE

    load_inv = pltpu.make_async_copy(inv_hbm, inv_ref, in_sem.at[0])
    load_inv.start()
    load_map = pltpu.make_async_copy(map_hbm, map_ref, in_sem.at[1])
    loads = []
    for s in range(4):
        rows = pl.ds(s * 256, 256)
        loads.append(pltpu.make_async_copy(coup_hbm.at[rows], coup_ref.at[rows], in_sem.at[3 + s]))
        loads[s].start()
    load_map.start()
    load_parent = pltpu.make_async_copy(parent_hbm, parent_ref, in_sem.at[2])
    load_parent.start()

    barrier = pltpu.get_barrier_semaphore()
    for dx in range(4):
        for dy in range(4):
            if dx or dy:
                pl.semaphore_signal(
                    barrier, inc=1,
                    device_id={"prow": nxt(ci, dx), "pcol": nxt(cj, dy)},
                    device_id_type=mesh_id)

    load_inv.wait()
    ih, il = split(inv_ref[...])
    for s in range(4):
        loads[s].wait()
        c = split(coup_ref[s * 256:s * 256 + 256, :])
        h, l = split(dot3(c, (ih, il)))
        for k in range(2):
            fac_h[2 * s + k] = h[k * BLK:k * BLK + BLK]
            fac_l[2 * s + k] = l[k * BLK:k * BLK + BLK]
    load_map.wait()
    load_parent.wait()

    def place(b):
        s = jnp.int32(0)
        found = jnp.int32(0)
        for k in range(8):
            hit = jnp.logical_and(map_ref[0, k] == b, blocks_ref[0] > k)
            s = jnp.where(hit, k, s)
            found = jnp.where(hit, 1, found)
        h = fac_h[s]
        l = fac_l[s]
        rows = pl.ds(pl.multiple_of(b * BLK, BLK), BLK)
        fh[rows, :] = jnp.where(found > 0, h, jnp.zeros_like(h))
        fl[rows, :] = jnp.where(found > 0, l, jnp.zeros_like(l))

    pl.loop(0, 4)(place)

    def tiles(col, lo, hi, base):
        @pl.loop(lo, hi)
        def _(r):
            rows = pl.ds(pl.multiple_of(r * TILE, TILE), TILE)
            cols = pl.ds(col * TILE, TILE)
            d = dot3((fh[rows, :], fl[rows, :]), (fh[cols, :], fl[cols, :]))
            if col == 0:
                mine = jnp.logical_and(ci == r, cj == 0)
                d = d - jnp.where(mine, parent_ref[...], jnp.zeros((TILE, TILE), F32))
            for c in range(2):
                for a in range(4):
                    o = c * 256 + a * 64
                    s_buf[c, a, base + r] = d[o:o + 64]
        if lo == col:
            t = base + col
            for a in range(2):
                s_buf[0, a, t, :, 256:384] = s_buf[1, a, t, :, 256:384]
                s_buf[0, a, t, :, 128:256] = s_buf[1, 2 + a, t, :, 384:512]
                s_buf[0, 2 + a, t, :, 256:384] = s_buf[1, 2 + a, t, :, 256:384]

    def remote(src, dst, ss, rs_, dev):
        return functools.partial(
            pltpu.make_async_remote_copy, src_ref=src, dst_ref=dst, send_sem=ss, recv_sem=rs_,
            device_id=dev, device_id_type=mesh_id)

    started = []

    def go(cp):
        cp().start()
        started.append(cp)

    STEP = (1, 3)

    def x_copy(stage, c, k, src, dst, axis):
        return remote(src, dst, xs_sem.at[stage, c, k - 1], xr_sem.at[stage, c, k - 1], {axis: nxt(coord[axis], k)})

    def x_list(stage):
        out = []
        for k in ((2, 1, 3) if stage < 3 else (1, 3)):
            for c in range(2):
                cols = pl.ds(0, PACK[c])
                m, n = coord[AXES[c]], coord[AXES[1 - c]]
                if stage == 0:
                    out.append(x_copy(0, c, k, s_buf.at[c, nxt(m, k), 0, :, cols], g1.at[c, k - 1, :, cols], AXES[c]))
                elif stage == 1:
                    rows = pl.ds(pl.multiple_of(nxt(n, k) * 16, 16), 16)
                    out.append(x_copy(1, c, k, s_buf.at[c, m, 0, rows, cols], g2.at[c, k - 1, :, cols], AXES[1 - c]))
                else:
                    if stage == 2:
                        ref, axis = w0.at[c, m, pl.ds(pl.multiple_of(n * 16, 16), 16), cols], AXES[1 - c]
                    else:
                        ref, axis = w0.at[c, m, :, cols], AXES[c]
                    out.append(x_copy(stage, c, k, ref, ref, axis))
        return out

    def x_start(stage):
        for cp in x_list(stage):
            go(cp)

    def x_forward(c, d, v):
        axis = AXES[c]
        me = coord[axis]
        ref = w0.at[c, nxt(me, v), pl.ds(d * 32, 32), pl.ds(0, PACK[c])]
        return remote(ref, ref, xf_send.at[c, d], xf_recv.at[c, d], {axis: nxt(me, STEP[d])})

    def x_relay():
        for c in range(2):
            for d in range(2):
                x_copy(3, c, (1, 3)[d], *[w0.at[c, nxt(coord[AXES[c]], (3, 1)[d]), :, pl.ds(0, PACK[c])]] * 2,
                       AXES[c])().wait_recv()
                go(x_forward(c, d, (3, 1)[d]))

    def x_last():
        for c in range(2):
            for d in range(2):
                x_forward(c, d, 2)().wait_recv()

    def x_wait(stage):
        for cp in x_list(stage):
            cp().wait_recv()
        for c in range(2):
            m, n = coord[AXES[c]], coord[AXES[1 - c]]
            w = PACK[c]
            if stage == 0:
                s_buf[c, m, 0, :, 0:w] = ((s_buf[c, m, 0, :, 0:w] + g1[c, 0, :, 0:w])
                                          + (g1[c, 1, :, 0:w] + g1[c, 2, :, 0:w]))
            elif stage == 1:
                rows = pl.ds(pl.multiple_of(n * 16, 16), 16)
                w0[c, m, rows, 0:w] = ((s_buf[c, m, 0, rows, 0:w] + g2[c, 0, :, 0:w])
                                       + (g2[c, 1, :, 0:w] + g2[c, 2, :, 0:w]))

    def rs(t, c):
        cols = pl.ds(0, width(t, c))
        axis = AXES[c]
        me = coord[axis]

        def chunk(d, h):
            return s_buf.at[c, d, t, pl.ds(h * 32, 32), cols]

        def mk(kind, src, dst, d):
            return remote(src, dst, send_sem.at[t - 1, c, d, kind], recv_sem.at[t - 1, c, d, kind],
                          {axis: nxt(me, STEP[d])})
        relay = [mk(0, chunk(nxt(me, 2), 1 - d), rl1.at[c, d, t, :, cols], d) for d in range(2)]
        raw = [mk(1, chunk(nxt(me, STEP[d]), d), rf1.at[c, d, t, pl.ds(d * 32, 32), cols], d) for d in range(2)]
        fin = [mk(2, chunk(nxt(me, STEP[d]), 1 - d), rf1.at[c, d, t, pl.ds((1 - d) * 32, 32), cols], d)
               for d in range(2)]
        return relay, raw, fin, chunk, me

    def second(t):
        out = []
        for k in (2, 1, 3):
            for c in range(2):
                cols = pl.ds(0, width(t, c))
                m, n = coord[AXES[c]], coord[AXES[1 - c]]
                rows = pl.ds(pl.multiple_of(nxt(n, k) * 16, 16), 16)
                out.append(remote(s_buf.at[c, m, t, rows, cols], rf2.at[c, k - 1, t, :, cols],
                                  send2_sem.at[t - 1, c, k - 1], recv2_sem.at[t - 1, c, k - 1],
                                  {AXES[1 - c]: nxt(n, k)}))
        return out

    def ev_a(t):
        for c in range(2):
            relay, raw = rs(t, c)[:2]
            for d in range(2):
                go(relay[d])
            for d in range(2):
                go(raw[d])

    def ev_b(t):
        for c in range(2):
            relay, raw, fin, chunk, me = rs(t, c)
            for d in range(2):
                relay[d]().wait_recv()
                ref = chunk(nxt(me, STEP[d]), 1 - d)
                ref[...] = ref[...] + rl1[c, d, t, :, 0:width(t, c)]
                go(fin[d])

    def ev_c(t):
        for c in range(2):
            w = width(t, c)
            relay, raw, fin, chunk, me = rs(t, c)
            for d in range(2):
                raw[d]().wait_recv()
                fin[d]().wait_recv()
            m = coord[AXES[c]]
            s_buf[c, m, t, :, 0:w] = s_buf[c, m, t, :, 0:w] + rf1[c, 0, t, :, 0:w] + rf1[c, 1, t, :, 0:w]
        for cp in second(t):
            go(cp)

    def ev_e(t):
        for cp in second(t):
            cp().wait_recv()
        for c in range(2):
            w = width(t, c)
            m, n = coord[AXES[c]], coord[AXES[1 - c]]
            rows = pl.ds(pl.multiple_of(n * 16, 16), 16)
            z_buf[c, t - 1, :, 0:w] = ((s_buf[c, m, t, rows, 0:w] + rf2[c, 0, t, :, 0:w])
                                       + (rf2[c, 1, t, :, 0:w] + rf2[c, 2, t, :, 0:w]))
        if t < 4:
            panel_send(t)
        else:
            deliver(t)

    guarded = []

    def go_unless(mine, cp):
        @pl.when(jnp.logical_not(mine))
        def _():
            cp().start()
        guarded.append((jnp.logical_not(mine), cp))

    def panel_send(t):
        for c in range(2):
            m, n = coord[AXES[c]], coord[AXES[1 - c]]
            rows = pl.ds(pl.multiple_of(n * 16, 16), 16)
            for k, (buf, axis) in enumerate(((wr, "prow"), (wc, "pcol"))):
                mine = coord[axis] == t

                @pl.when(mine)
                def _():
                    buf[c, m, rows, :] = z_buf[c, t - 1]
                go_unless(mine, remote(z_buf.at[c, t - 1], buf.at[c, m, rows], pa_send.at[t - 1, c, k], pa_recv.at[k], {axis: t}))

    def ring(k):
        buf, axis = ((wr, "pcol"), (wc, "prow"))[k]
        me = coord[axis]

        def part(v, c, h, n):
            if c != k:
                return buf.at[c, v, pl.ds(h * 32, n * 32)]
            return buf.at[c, pl.ds(h * 2, n * 2), pl.ds(pl.multiple_of(v * 16, 16), 16)]
        res = []
        for c in range(2):
            for d in range(2):
                def mk(kind, ref):
                    return remote(ref, ref, pb_send.at[k, c, d, kind], pb_recv.at[k, c, d, kind], {axis: nxt(me, STEP[d])})
                prev = nxt(me, STEP[1 - d])
                res.append((mk(0, part(me, c, 0, 2)), mk(0, part(prev, c, 0, 2)),
                            mk(1, part(prev, c, d, 1)), mk(1, part(nxt(me, 2), c, d, 1))))
        return res

    def panel_stage(stage):
        for k in range(2):
            @pl.when((ci, cj)[k] > 0)
            def _():
                if stage == 0:
                    got = (wr, wc)[k].at[0, pl.ds(0, 3), pl.ds(0, 32)]
                    pltpu.make_async_copy(got, got, pa_recv.at[k]).wait()
                for own, own_in, fwd, fwd_in in ring(k):
                    if stage == 0:
                        own().start()
                    elif stage == 1:
                        own_in().wait_recv()
                        fwd().start()
                    elif stage == 2:
                        fwd_in().wait_recv()
                    else:
                        own().wait_send()
                        fwd().wait_send()

    def deliver(t):
        r, q = OWNERS[t - 4]
        for k, (x, y) in enumerate(((r, q), (q, r))[: 1 if r == q else 2]):
            mine = jnp.logical_and(ci == x, cj == y)
            for c in range(2):
                cols = pl.ds(0, width(t, c))
                m, v = coord[AXES[c]], coord[AXES[1 - c]]
                rows = pl.ds(pl.multiple_of(c * 256 + m * 64 + v * 16, 16), 16)

                @pl.when(mine)
                def _():
                    t_buf[rows, cols] = z_buf[c, t - 1, :, cols]
                go_unless(mine, remote(z_buf.at[c, t - 1, :, cols], t_buf.at[rows, cols], dist_send.at[t - 4, k, c],
                                       dist_recv.at[0], {"prow": x, "pcol": y}))

    def chol_begin(kb):
        o = kb * BLK
        eye = lax.broadcasted_iota(jnp.int32, (BLK, BLK), 0) == lax.broadcasted_iota(jnp.int32, (BLK, BLK), 1)
        md[:, 0:BLK] = ch[o:o + BLK, o:o + BLK]
        md[:, BLK:2 * BLK] = eye.astype(F32)

    def chol_chunk(q):
        lo = q * 32
        x = md[lo:BLK, 0:BLK]
        y = md[lo:BLK, BLK:2 * BLK]
        rid = lax.broadcasted_iota(jnp.int32, (BLK - lo, BLK), 0)
        for k in range(0, 32, 2):
            c0 = jnp.broadcast_to(x[:, lo + k:lo + k + 1], x.shape)
            c1 = jnp.broadcast_to(x[:, lo + k + 1:lo + k + 2], x.shape)
            a = c0[k:k + 1, :]
            b = c0[k + 1:k + 2, :]
            d = c1[k + 1:k + 2, :]
            ia = 1.0 / a
            ba = b * ia
            s = d - b * ba
            isv = 1.0 / s
            m0 = jnp.where(rid > k + 1, c0, 0.0)
            m1 = jnp.where(rid > k + 1, c1, 0.0) - m0 * ba
            m0 = jnp.where(rid == k + 1, b, m0)
            xa = x[k:k + 1, :]
            ya = y[k:k + 1, :]
            xb = (x[k + 1:k + 2, :] - ba * xa) * isv
            yb = (y[k + 1:k + 2, :] - ba * ya) * isv
            xa = xa * ia
            ya = ya * ia
            x = x - m0 * xa - m1 * xb
            y = y - m0 * ya - m1 * yb
        md[lo:BLK, 0:BLK] = x
        md[lo:BLK, BLK:2 * BLK] = y

    def chol_end(kb):
        o = kb * BLK
        ri = lax.broadcasted_iota(jnp.int32, (BLK, BLK), 0)
        cj_ = lax.broadcasted_iota(jnp.int32, (BLK, BLK), 1)
        u = md[:, 0:BLK]
        piv = jnp.sum(jnp.where(ri == cj_, u, 0.0), axis=1, keepdims=True)
        sc = lax.rsqrt(piv)
        li = md[:, BLK:2 * BLK] * sc
        linv[kb] = li
        low = jnp.where(cj_ >= ri, u * sc, 0.0).T
        ch[o:o + BLK, o:o + BLK] = low
        if kb < 3:
            lp = lax.dot_general(ch[o + BLK:, o:o + BLK], li, DN_NT, precision=lax.Precision.HIGHEST,
                                 preferred_element_type=F32)
            ch[o + BLK:, o:o + BLK] = lp
            ch[o + BLK:, o + BLK:] = ch[o + BLK:, o + BLK:] - lax.dot_general(
                lp, lp, DN_NT, precision=lax.Precision.HIGHEST, preferred_element_type=F32)
            ch[o:o + BLK, o + BLK:] = jnp.zeros((BLK, TILE - o - BLK), F32)

    def solve(x, buf):
        @pl.loop(0, 2)
        def _(c):
            a = -jnp.reshape(buf[c], (256, TILE))
            rows = pl.ds(pl.multiple_of(c * 256, 256), 256)
            for b in range(4):
                o = b * BLK
                v = a[:, o:o + BLK]
                if b:
                    v = v - mm_nt(p_buf[x, rows, 0:o], ch[o:o + BLK, 0:o])
                p_buf[x, rows, o:o + BLK] = mm_nt(v, linv[b])

    tiles(0, 0, 1, 0)
    pl.semaphore_wait(barrier, 15)
    x_start(0)
    pl.loop(4, 16)(place)
    tiles(0, 1, 4, 0)
    ev_a(1)
    x_wait(0)
    x_start(1)
    ev_a(2)
    tiles(1, 1, 4, 3)
    x_wait(1)
    x_start(2)
    ev_b(1)
    ev_a(3)
    x_wait(2)
    x_start(3)
    ev_b(2)
    ev_a(4)
    tiles(2, 2, 4, 5)
    tiles(3, 3, 4, 6)
    ev_c(1)
    x_relay()

    fn = {"a": ev_a, "b": ev_b, "c": ev_c, "e": ev_e, "p": panel_stage}
    order = ("c2 e1 b4", "a6 c3 e2", "b5 a7 c4", "e3 b6 a8", "c5 p0 e4", "b7 a9 c6", "p1 e5 b8", "c7 p2 e6",
             "b9 c8 e7", "c9 e8 e9")
    order = [w for part in order for w in part.split()]
    head = 26
    ev_b(3)
    ev_a(5)
    x_last()
    ch[...] = jnp.zeros((TILE, TILE), F32)
    for a in range(4):
        o = a * 64
        n = 128 * (1 + a // 2)
        ch[o:o + 64, 0:n] = -w0[0, a, :, 0:n]
        ch[256 + o:320 + o, 0:256] = -w0[1, a, :, 0:256]
        ch[256 + o:320 + o, 256:384] = -w0[0, a, :, 256:384]
    for a in range(2):
        ch[384 + a * 64:448 + a * 64, 384:512] = -w0[0, a, :, 128:256]

    at = 0
    for kb in range(4):
        chol_begin(kb)
        for q in range(4):
            upto = (head * (4 * kb + q + 1)) // 16
            while at < upto:
                fn[order[at][0]](int(order[at][1]))
                at += 1
            chol_chunk(q)
        chol_end(kb)

    trail = jnp.logical_and(ci > 0, cj > 0)
    for n, w in enumerate(order[head:]):
        fn[w[0]](int(w[1]))
        if n == 1:
            @pl.when(ci > 0)
            def _():
                solve(0, wr)
        if n == 3:
            @pl.when(trail)
            def _():
                solve(1, wc)

                @pl.loop(0, 2)
                def _(c):
                    rows = pl.ds(pl.multiple_of(c * 256, 256), 256)
                    out_ref[rows, :] = parent_ref[rows, :] - mm_nt(p_buf[0, rows, :], p_buf[1])

    def arrived(rows, w):
        done = t_buf.at[pl.ds(0, rows), pl.ds(0, w)]
        pltpu.make_async_copy(done, done, dist_recv.at[0]).wait()

    @pl.when(jnp.logical_and(trail, ci == cj))
    def _():
        arrived(400, 384)
        for p in range(4):
            for q in range(p + 1):
                y, x = {(2, 2): (0, 2), (3, 2): (1, 2), (3, 3): (0, 1)}.get((p, q), (p, q))
                v = t_buf[y * BLK:(y + 1) * BLK, x * BLK:(x + 1) * BLK]
                out_ref[p * BLK:(p + 1) * BLK, q * BLK:(q + 1) * BLK] -= v
                if p != q:
                    out_ref[q * BLK:(q + 1) * BLK, p * BLK:(p + 1) * BLK] -= v.T

    @pl.when(jnp.logical_and(trail, ci > cj))
    def _():
        arrived(480, TILE)
        out_ref[...] = out_ref[...] - t_buf[...]

    @pl.when(jnp.logical_and(trail, ci < cj))
    def _():
        arrived(480, TILE)
        for b in range(4):
            o = b * BLK
            out_ref[:, o:o + BLK] = out_ref[:, o:o + BLK] - t_buf[o:o + BLK, :].T

    @pl.when(jnp.logical_and(ci > 0, cj == 0))
    def _():
        out_ref[...] = p_buf[0]

    @pl.when(jnp.logical_and(ci == 0, cj == 0))
    def _():
        out_ref[...] = ch[...]

    @pl.when(jnp.logical_and(ci == 0, cj > 0))
    def _():
        for c in range(2):
            for a in range(2):
                o = c * 256 + a * 128
                out_ref[:, o:o + BLK] = -(jnp.reshape(wc[c, 2 * a:2 * a + 2], (BLK, TILE)).T)

    for cp in started:
        cp().wait_send()
    panel_stage(3)
    for cond, cp in guarded:
        @pl.when(cond)
        def _():
            cp().wait_send()


def body(child_inverse, child_coupling, child_blocks, child_map, parent_front):
    vm = pltpu.VMEM
    dma = pltpu.SemaphoreType.DMA
    return pl.pallas_call(
        kernel,
        out_shape=jax.ShapeDtypeStruct((TILE, TILE), F32),
        in_specs=[pl.BlockSpec(memory_space=pltpu.SMEM if k == 1 else pltpu.HBM) for k in range(5)],
        out_specs=pl.BlockSpec(memory_space=vm),
        scratch_shapes=[
            pltpu.SMEM((1, 8), jnp.int32), vm((TILE, TILE), F32), vm((1024, TILE), F32), vm((TILE, TILE), F32), dma((7,)),
            vm((8, BLK, TILE), BF16), vm((8, BLK, TILE), BF16),
            vm((2048, TILE), BF16), vm((2048, TILE), BF16),
            vm((2, 4, NT, 64, TILE), F32),
            vm((2, 2, NT, 32, TILE), F32), vm((2, 2, NT, 64, TILE), F32),
            vm((2, 3, NT, 16, TILE), F32),
            vm((2, 3, 64, 384), F32), vm((2, 3, 16, 384), F32), vm((2, 4, 64, 384), F32),
            vm((2, 4, 64, TILE), F32), vm((2, 4, 64, TILE), F32),
            vm((2, 9, 16, TILE), F32), vm((TILE, TILE), F32),
            vm((TILE, TILE), F32), vm((BLK, 2 * BLK), F32), vm((4, BLK, BLK), F32), vm((2, TILE, TILE), F32),
            dma((9, 2, 2, 3)), dma((9, 2, 2, 3)), dma((9, 2, 3)), dma((9, 2, 3)), dma((4, 2, 3)), dma((4, 2, 3)), dma((2, 2)), dma((2, 2)),
            dma((3, 2, 2)), dma((2,)), dma((2, 2, 2, 2)), dma((2, 2, 2, 2)), dma((6, 2, 2)), dma((1,)),
        ],
        compiler_params=pltpu.CompilerParams(collective_id=0, has_side_effects=True, vmem_limit_bytes=60 * 1024 * 1024),
    )(child_map, child_blocks, child_inverse[0], child_coupling[0], parent_front)


def solution(mesh):
    return jax.shard_map(
        body,
        mesh=mesh,
        in_specs=(
            P(("leaf", "prow", "pcol"), None, None),
            P(("leaf", "prow", "pcol"), None, None),
            P(("leaf", "prow", "pcol")),
            P(("leaf", "prow", "pcol"), None),
            P(("leaf", "prow"), "pcol"),
        ),
        out_specs=P(("leaf", "prow"), "pcol"),
        check_vma=False,
    )
```
